512 devices in a mesh: row: 32 (over z, y_hi), col: 16 (over x, y_lo, core).
Axes of the slice: x: 4, y: 8 (y_hi: 4, y_lo: 2; y = y_hi * 2 + y_lo), z: 8, core: 2. Of those that a mesh axis runs over, the one named last changes fastest.
Arguments:
- vectors: float32 [16384, 2048], P('row', 'col'), may hold values from -6 to 6
- reflectors: float32 [32, 1024, 512], P('row', 'col'), may hold values from -2 to 2
- factors: float32 [32, 512, 512], P('row', 'col'), may hold values from -2 to 2
Outputs:
- transformed: float32 [16384, 2048], P('row', 'col')
The draws below stay inside these ranges and needn't reach their ends.
All inputs are finite; a program needn't handle non-finite values.
Results may differ from the reference program's by a relative error of at most 0.0003.
Values sent between devices are 32-bit elements; how exact they have to be, the bound alone decides.
No kernel may reach another device: no remote copies, remote signals or barrier semaphores. Data moves between devices by JAX's collectives and lax.ppermute only.
A program may use at most 64 MiB of HBM per device.

```python
import math
import jax
import jax.numpy as jnp
from jax import lax

BAND = 512
NBLK = 32
ROWS = 16384
EIGENS = 2048


def reflector_set(key):
    base = jax.random.fold_in(key, 11)
    upper_key, skew_key, ratio_key = jax.random.split(base, 3)
    spread = 0.25
    wobble = 0.05
    row_index = lax.broadcasted_iota(jnp.int32, (NBLK, BAND, BAND), 1)
    col_index = lax.broadcasted_iota(jnp.int32, (NBLK, BAND, BAND), 2)
    block_index = lax.broadcasted_iota(jnp.int32, (NBLK, BAND, BAND), 0)
    noise = jnp.clip(jax.random.normal(upper_key, (NBLK, BAND, BAND), jnp.float32), -4.0, 4.0)
    noise = noise * (spread / math.sqrt(BAND))
    upper = jnp.where(row_index == col_index, 1.0, jnp.where(row_index > col_index, noise, 0.0))
    upper = upper.astype(jnp.float32)
    upper_norm = jnp.sqrt(jnp.sum(upper * upper, axis=1, keepdims=True))
    raw = jax.random.normal(skew_key, (NBLK, BAND, BAND), jnp.float32) * (math.sqrt(2.0) / math.sqrt(BAND))
    skew = (raw - jnp.swapaxes(raw, 1, 2)) * math.sqrt(0.5)
    identity = jnp.eye(BAND, dtype=jnp.float32)
    rotation = jnp.linalg.solve(identity[None] + skew, identity[None] - skew)
    ratio = jax.random.uniform(ratio_key, (NBLK, 1, BAND), jnp.float32, 1.0 - wobble, 1.0 + wobble)
    lower = rotation * (upper_norm * ratio)
    lower = jnp.where(block_index == NBLK - 1, 0.0, lower)
    shaped = jnp.concatenate([upper, lower], axis=1).astype(jnp.float32)
    gram = jnp.einsum('kij,kil->kjl', shaped, shaped, precision=lax.Precision.HIGHEST)
    half_diagonal = jnp.diagonal(gram, axis1=1, axis2=2)[:, :, None] * identity[None] * 0.5
    inverse_factor = jnp.triu(gram, 1) + half_diagonal
    right_sides = jnp.broadcast_to(identity[None], (NBLK, BAND, BAND))
    triangle = lax.linalg.triangular_solve(inverse_factor, right_sides, left_side=True, lower=False)
    return (shaped, triangle.astype(jnp.float32))


def draw_reflectors(key, part):
    return reflector_set(key)[0]


def draw_factors(key, part):
    return reflector_set(key)[1]


def steps_of(stream_key, shape, cuts, low, top_value):
    loudness, own = 1.0, jax.random.fold_in(stream_key, 6)
    for position, parts in cuts:
        heights = jnp.exp(jax.random.uniform(jax.random.fold_in(own, position), (parts,), jnp.float32, low / len(cuts), top_value / len(cuts)))
        loudness = loudness * jnp.repeat(heights, shape[position] // parts).reshape([-1 if axis == position else 1 for axis in range(len(shape))])
    return loudness


def centred(stream_key, shape, scale, limit, cuts=(), kind=jnp.bfloat16):
    drawn = jax.random.normal(stream_key, shape, jnp.float32) * scale
    if len(cuts) > 0:
        drawn = steps_of(stream_key, shape, cuts, -0.22, 0.18) * drawn
    return jnp.clip(drawn, min=-limit, max=limit).astype(kind)


def setup_inputs(seed: int = 0) -> dict:
    keys = jax.random.split(jax.random.key(seed), 4)
    return {
        "vectors": centred(keys[0], (ROWS, EIGENS), 1.0, 6.0, ((0, 32), (1, 16)), jnp.float32),
        "reflectors": draw_reflectors(jax.random.fold_in(keys[3], 71), 0),
        "factors": draw_factors(jax.random.fold_in(keys[3], 71), 0),
    }


def product(left, right):
    return jnp.dot(left.astype(jnp.float32), right.astype(jnp.float32), precision=lax.Precision.HIGHEST, preferred_element_type=jnp.float32)

def reference(vectors, reflectors, factors):
    block_count = reflectors.shape[0]
    band_rows = factors.shape[1]
    padded = jnp.concatenate([vectors, jnp.zeros((band_rows, vectors.shape[1]), vectors.dtype)], axis=0)

    def apply_block(turn, field):
        block = (block_count - 1 - turn).astype(jnp.int32)
        start = (block * band_rows).astype(jnp.int32)
        window = lax.dynamic_slice_in_dim(field, start, 2 * band_rows, 0)
        shaped = lax.dynamic_index_in_dim(reflectors, block, 0, keepdims=False)
        triangle = lax.dynamic_index_in_dim(factors, block, 0, keepdims=False)
        updated = window - product(shaped, product(triangle, product(shaped.T, window)))
        return lax.dynamic_update_slice_in_dim(field, updated, start, 0)
    padded = lax.fori_loop(jnp.int32(0), jnp.int32(block_count), apply_block, padded)
    return padded[:block_count * band_rows]
```

```python
import jax
import jax.numpy as jnp
from jax import lax
from jax.sharding import Mesh
from jax.sharding import PartitionSpec as P

ROW = ("z", "h")
COL = ("x", "l", "c")


def dot(a, b, da, db):
    return lax.dot_general(
        a, b, (((da,), (db,)), ((), ())), precision=lax.Precision.HIGH, preferred_element_type=jnp.float32
    )


def spread(part, axes):
    count = lax.axis_size(axes)
    return lax.all_to_all(jnp.broadcast_to(part[None], (count, *part.shape)), axes, 0, 0)


def swapped(value):
    return lax.ppermute(value, "c", [(0, 1), (1, 0)])


def both_halves(own, core, dim):
    other = swapped(own)
    first = jnp.where(core == 0, own, other)
    second = jnp.where(core == 0, other, own)
    return jnp.stack([first, second], axis=dim)


def local(vectors, reflectors, factors):
    planes, rows = lax.axis_size("z"), lax.axis_size("h")
    core = lax.axis_index("c")
    band = factors.shape[2]
    shard = jnp.concatenate([reflectors[0], factors[0]], axis=0)
    strip = reflectors.shape[1]
    blocks = both_halves(spread(shard, ("x", "l")), core, 1)
    shaped = blocks[:, :, :strip].reshape(2 * band, band)
    triangle = blocks[:, :, strip:].reshape(band, band)
    upper, lower = shaped[:band], shaped[band:]
    inner = dot(dot(vectors, upper, 0, 0), triangle, 1, 1)
    edge = vectors.T - dot(inner, upper, 1, 1)
    reach = dot(triangle, lower, 1, 1)
    coupling = -dot(upper, reach, 1, 0)
    chips = lax.axis_size(("x", "l"))
    height = band // (2 * chips)
    here = core * chips + lax.axis_index(("x", "l"))
    own = lax.dynamic_slice_in_dim(coupling, here * height, height, 0)
    width = edge.shape[0] // rows
    sent = jnp.concatenate(
        [jnp.broadcast_to(own[None], (rows, height, band)), edge.reshape(rows, width, band)], axis=1
    )
    got = lax.all_to_all(sent, "h", 0, 0)
    edges = got[:, height:]
    couplings = both_halves(spread(got[:, :height], ("x", "l")).transpose(1, 0, 2, 3), core, 1)
    couplings = couplings.reshape(rows, band, band)
    total, bottom = couplings[rows - 1], edges[rows - 1]
    for k in reversed(range(rows - 1)):
        bottom = edges[k] + dot(bottom, couplings[k], 1, 1)
        total = dot(couplings[k], total, 1, 0)
    top, below = bottom, jnp.zeros_like(bottom)
    for k in reversed(range(1, planes)):
        came = lax.ppermute(top, "z", [(k, k - 1)])
        top = top + dot(came, total, 1, 1)
        below = below + came
    tops = [below]
    for k in reversed(range(1, rows)):
        tops.insert(0, edges[k] + dot(tops[0], couplings[k], 1, 1))
    under = lax.all_to_all(jnp.stack(tops), "h", 0, 0).reshape(rows * width, band)
    mixed = inner + dot(under, reach, 1, 1)
    lowest = under.T - dot(lower, mixed, 1, 1)
    upmost = vectors - dot(upper, mixed, 1, 1)
    count = planes * rows
    moved = lax.ppermute(lowest, ROW, [(k, k + 1) for k in range(count - 1)])
    return jnp.where(lax.axis_index(ROW) == 0, upmost, moved)


def solution(mesh):
    split = Mesh(mesh.devices.reshape(8, 4, 4, 2, 2), ROW + COL)
    return jax.shard_map(
        local,
        mesh=split,
        in_specs=(P(ROW, COL), P(ROW, COL, None), P(ROW, COL, None)),
        out_specs=P(ROW, COL),
        check_vma=False,
    )
```

```python
import jax
import jax.numpy as jnp
from jax import lax
from jax.sharding import Mesh
from jax.sharding import PartitionSpec as P

ROW = ("z", "h")
COL = ("x", "l", "c")


def dot(a, b, da, db):
    return lax.dot_general(
        a, b, (((da,), (db,)), ((), ())), precision=lax.Precision.HIGH, preferred_element_type=jnp.float32
    )


def spread(part, axes):
    count = lax.axis_size(axes)
    return lax.all_to_all(jnp.broadcast_to(part[None], (count, *part.shape)), axes, 0, 0)


def both_halves(own, core, dim):
    other = lax.ppermute(own, "c", [(0, 1), (1, 0)])
    first = jnp.where(core == 0, own, other)
    second = jnp.where(core == 0, other, own)
    return jnp.stack([first, second], axis=dim)


def pick(choices, which):
    value = choices[-1]
    for k in reversed(range(len(choices) - 1)):
        if choices[k] is not value:
            value = jnp.where(which == k, choices[k], value)
    return value


def transformed(vectors, reflectors, factors):
    planes, rows = lax.axis_size("z"), lax.axis_size("h")
    core, place = lax.axis_index("c"), lax.axis_index("h")
    band, strip = factors.shape[2], reflectors.shape[1]
    part = spread(jnp.concatenate([reflectors[0], factors[0]], axis=0), ("x", "l"))
    blocks = both_halves(part, core, 1)
    shaped = blocks[:, :, :strip].reshape(2 * band, band)
    triangle = blocks[:, :, strip:].reshape(band, band)
    upper, lower = shaped[:band], shaped[band:]
    chips = lax.axis_size(("x", "l"))
    height = band // (2 * chips)
    here = core * chips + lax.axis_index(("x", "l"))
    own = -dot(dot(lax.dynamic_slice_in_dim(upper, here * height, height, 0), triangle, 1, 0), lower, 1, 1)
    shards = spread(own, "h")
    reach = dot(triangle, lower, 1, 1)
    inner = dot(dot(vectors, upper, 0, 0), triangle, 1, 1)
    edge = vectors.T - dot(inner, upper, 1, 1)
    width = edge.shape[0] // rows
    slices, edges = edge.reshape(rows, width, band), []
    for s in range(rows):
        piece = lax.dynamic_index_in_dim(slices, (place - s) % rows, 0, keepdims=False)
        above = [(k, (k - s) % rows) for k in range(rows)]
        edges.append(lax.ppermute(piece, "h", above) if s else piece)
    edges = [pick([edges[(k - h) % rows] for h in range(rows)], place) for k in range(rows)]
    coupling = lax.optimization_barrier(-dot(upper, reach, 1, 0))
    others = [jnp.where(place <= k, shards[k + 1], shards[k]) for k in range(rows - 1)]
    part = spread(jnp.stack(others), ("x", "l"))
    halves = both_halves(part, core, 0).transpose(2, 0, 1, 3, 4).reshape(rows - 1, band, band)
    couplings = [
        pick([halves[k - 1] if k > h else coupling if k == h else halves[k] for h in range(rows)], place)
        for k in range(rows)
    ]
    count = planes * rows
    down = [(k, k + 1) for k in range(count - 1)]
    pull = dot(lower, reach, 1, 0)
    pull = lax.dynamic_slice_in_dim(pull, core * (band // 2), band // 2, 0)
    extra = jnp.concatenate([pull, dot(inner, lower, 1, 1)])
    extra = lax.ppermute(extra, ROW, down)
    pull, fixed = both_halves(extra[: band // 2], core, 0).reshape(band, band), extra[band // 2 :]
    total, bottom = couplings[rows - 1], edges[rows - 1]
    for k in reversed(range(rows - 1)):
        bottom = edges[k] + dot(bottom, couplings[k], 1, 1)
        total = dot(couplings[k], total, 1, 0)
    top, below = bottom, jnp.zeros_like(bottom)
    for k in reversed(range(1, planes)):
        came = lax.ppermute(top, "z", [(k, k - 1)])
        top = top + dot(came, total, 1, 1)
        below = below + came
    tops = [below]
    for k in reversed(range(1, rows)):
        tops.insert(0, edges[k] + dot(tops[0], couplings[k], 1, 1))
    mine = jnp.stack([top, *tops[:-1]])
    mine = lax.all_to_all(mine, "h", 0, 0).reshape(rows * width, band)
    return mine.T - dot(pull, mine, 1, 1) - fixed.T


def solution(mesh):
    split = Mesh(mesh.devices.reshape(8, 4, 4, 2, 2), ROW + COL)
    return jax.shard_map(
        transformed,
        mesh=split,
        in_specs=(P(ROW, COL), P(ROW, COL, None), P(ROW, COL, None)),
        out_specs=P(ROW, COL),
        check_vma=False,
    )
```

```python
import jax
import jax.numpy as jnp
from jax import lax
from jax.sharding import Mesh
from jax.sharding import PartitionSpec as P

ROW = ("z", "h")
COL = ("x", "l", "c")


def dot(a, b, da, db):
    return lax.dot_general(
        a, b, (((da,), (db,)), ((), ())), precision=lax.Precision.HIGH, preferred_element_type=jnp.float32
    )


def spread(part, axes):
    count = lax.axis_size(axes)
    return lax.all_to_all(jnp.broadcast_to(part[None], (count, *part.shape)), axes, 0, 0)


def both_halves(own, core, dim):
    other = lax.ppermute(own, "c", [(0, 1), (1, 0)])
    first = jnp.where(core == 0, own, other)
    second = jnp.where(core == 0, other, own)
    return jnp.stack([first, second], axis=dim)


def pick(choices, which):
    value = choices[-1]
    for k in reversed(range(len(choices) - 1)):
        if choices[k] is not value:
            value = jnp.where(which == k, choices[k], value)
    return value


def transformed(vectors, reflectors, factors):
    planes, rows = lax.axis_size("z"), lax.axis_size("h")
    core, place = lax.axis_index("c"), lax.axis_index("h")
    band, strip = factors.shape[2], reflectors.shape[1]
    part = spread(jnp.concatenate([reflectors[0], factors[0]], axis=0), ("x", "l"))
    blocks = both_halves(part, core, 1)
    shaped = blocks[:, :, :strip].reshape(2 * band, band)
    triangle = blocks[:, :, strip:].reshape(band, band)
    upper, lower = shaped[:band], shaped[band:]
    chips = lax.axis_size(("x", "l"))
    height = band // (2 * chips)
    here = core * chips + lax.axis_index(("x", "l"))
    own = -dot(dot(lax.dynamic_slice_in_dim(upper, here * height, height, 0), triangle, 1, 0), lower, 1, 1)
    shards = spread(own, "h")
    reach = dot(triangle, lower, 1, 1)
    coupling = lax.optimization_barrier(-dot(upper, reach, 1, 0))
    inner = dot(dot(vectors, upper, 0, 0), triangle, 1, 1)
    edge = vectors.T - dot(inner, upper, 1, 1)
    width = edge.shape[0] // rows
    slices, edges = edge.reshape(rows, width, band), []
    for s in range(rows):
        piece = lax.dynamic_index_in_dim(slices, (place - s) % rows, 0, keepdims=False)
        above = [(k, (k - s) % rows) for k in range(rows)]
        edges.append(lax.ppermute(piece, "h", above) if s else piece)
    edges = [pick([edges[(k - h) % rows] for h in range(rows)], place) for k in range(rows)]
    others = [jnp.where(place <= k, shards[k + 1], shards[k]) for k in range(rows - 1)]
    part = spread(jnp.stack(others), ("x", "l"))
    halves = both_halves(part, core, 0).transpose(2, 0, 1, 3, 4).reshape(rows - 1, band, band)
    couplings = [
        pick([halves[k - 1] if k > h else coupling if k == h else halves[k] for h in range(rows)], place)
        for k in range(rows)
    ]
    count = planes * rows
    down = [(k, k + 1) for k in range(count - 1)]
    pull = dot(lower, reach, 1, 0)
    pull = lax.dynamic_slice_in_dim(pull, core * (band // 2), band // 2, 0)
    extra = jnp.concatenate([pull, dot(lower, inner, 1, 1).reshape(-1, band)])
    extra = lax.ppermute(extra, ROW, down)
    pull = both_halves(extra[: band // 2], core, 0).reshape(band, band)
    fixed = extra[band // 2 :].reshape(band, -1)
    total, bottom = couplings[rows - 1], edges[rows - 1]
    for k in reversed(range(rows - 1)):
        bottom = edges[k] + dot(bottom, couplings[k], 1, 1)
        total = dot(couplings[k], total, 1, 0)
    top, below = bottom, jnp.zeros_like(bottom)
    for k in reversed(range(1, planes)):
        came = lax.ppermute(top, "z", [(k, k - 1)])
        top = top + dot(came, total, 1, 1)
        below = below + came
    tops = [below]
    for k in reversed(range(1, rows)):
        tops.insert(0, edges[k] + dot(tops[0], couplings[k], 1, 1))
    mine = jnp.stack([top, *tops[:-1]])
    mine = lax.all_to_all(mine, "h", 0, 0).reshape(rows * width, band)
    return mine.T - dot(pull, mine, 1, 1) - fixed


def solution(mesh):
    split = Mesh(mesh.devices.reshape(8, 4, 4, 2, 2), ROW + COL)
    return jax.shard_map(
        transformed,
        mesh=split,
        in_specs=(P(ROW, COL), P(ROW, COL, None), P(ROW, COL, None)),
        out_specs=P(ROW, COL),
        check_vma=False,
    )
```
